256 devices in a mesh: ta: 16 (over y, x), sa: 16 (over z, core).
Axes of the slice: x: 4, y: 4, z: 8, core: 2. Of those that a mesh axis runs over, the one named last changes fastest.
Arguments:
- perambulator: bfloat16 [2, 16, 16, 384, 384], P(None, None, 'sa', 'ta'), may hold values from -6 to 6
- meson_ops: bfloat16 [2, 8, 16, 384, 384], P(None, None, 'ta'), may hold values from -0.21875 to 0.21875
- diagram_lists: int32 [16, 128, 2], P('ta', 'sa'), may hold values from 0 to 127, as said below
Outputs:
- correlators: float32 [2, 16, 16, 384, 384], P(None, 'ta', 'sa')
The draws below stay inside these ranges and needn't reach their ends.
Inputs may be any that keep to these rules, and one draw needn't show every extreme that they name: `diagram_lists`: every id lies in 0 to 127. Among the 16 ids of one owner's list, no spin pair (id // 8) occurs more than 2 times, and at least one spin pair occurs exactly 2 times; several may.
All inputs are finite; a program needn't handle non-finite values.
Results may differ from the reference program's by a relative error of at most 0.004.
Values may be sent and summed in bfloat16 or wider, within the bound.
No kernel may reach another device: no remote copies, remote signals or barrier semaphores. Data moves between devices by JAX's collectives and lax.ppermute only.
A program may use at most 128 MiB of HBM per device.

```python
import jax
import jax.numpy as jnp
from jax import lax

NEV = 384
OPS = 8
PAIRS = 8
CAP = 2
TS = 16
SPIN = 16
OWNERS = 16


def owner_list(key):
    key_hot, key_perm, key_order, key_ops = jax.random.split(key, 4)
    hot_spin = jax.random.randint(key_hot, (), 0, SPIN)
    shuffled = jax.random.permutation(key_perm, (SPIN - 1) * CAP)
    others = shuffled[:2 * PAIRS - CAP] // CAP
    others = others + (others >= hot_spin).astype(jnp.int32)
    spin_ids = jnp.concatenate([jnp.full((CAP,), hot_spin, jnp.int32), others.astype(jnp.int32)])
    order = jax.random.permutation(key_order, 2 * PAIRS)
    spin_ids = spin_ids[order]
    op_ids = jax.random.randint(key_ops, (2 * PAIRS,), 0, OPS)
    return (spin_ids * OPS + op_ids).astype(jnp.int32).reshape(PAIRS, 2)


def draw_diagram_lists(key, part):
    keys = jax.random.split(jax.random.fold_in(key, 7), TS * OWNERS)
    lists = jax.vmap(owner_list)(keys)
    return lists.reshape(TS, OWNERS * PAIRS, 2)


def level_of(stream_key, dims, cuts, smallest, largest):
    def one(axis_at, parts):
        draws = jax.random.uniform(jax.random.fold_in(jax.random.fold_in(stream_key, 6), axis_at), (parts,), jnp.float32, smallest / len(cuts), largest / len(cuts))
        return jnp.repeat(jnp.exp(draws), dims[axis_at] // parts).reshape((-1,) + (1,) * (len(dims) - axis_at - 1))

    factor_of = one(*cuts[0])
    for cut in cuts[1:]:
        factor_of = factor_of * one(*cut)
    return factor_of


def scatter_about(rng, dims, deviation, reach, shards=(), dtype=jnp.bfloat16):
    drawn = deviation * jax.random.normal(rng, dims, jnp.float32)
    if shards:
        drawn = drawn * level_of(rng, dims, shards, -0.22, 0.18)
    return jnp.clip(drawn, -reach, reach).astype(dtype)


def setup_inputs(seed: int = 0) -> dict:
    arg_keys = jax.random.split(jax.random.key(seed), 4)
    perambulator = scatter_about(arg_keys[0], (2, TS, SPIN, NEV, NEV), 1.0, 6.0, ((2, 16), (3, 16)))
    meson_ops = scatter_about(arg_keys[1], (2, OPS, TS, NEV, NEV), (2 * NEV) ** -0.5, 0.21875, ((2, 16),))
    diagram_lists = draw_diagram_lists(jax.random.fold_in(arg_keys[3], 71), 0)
    return dict(perambulator=perambulator, meson_ops=meson_ops, diagram_lists=diagram_lists)


def one_time(inputs):
    peram_time, ops_time, lists_time = inputs
    op_real = ops_time[0].astype(jnp.float32)
    op_imag = ops_time[1].astype(jnp.float32)
    pr_real = peram_time[0].astype(jnp.float32)
    pr_imag = peram_time[1].astype(jnp.float32)
    block_real = jnp.einsum('oik,sjk->soij', op_real, pr_real) - jnp.einsum('oik,sjk->soij', op_imag, pr_imag)
    block_imag = jnp.einsum('oik,sjk->soij', op_real, pr_imag) + jnp.einsum('oik,sjk->soij', op_imag, pr_real)
    blocks = jnp.stack([block_real, block_imag]).astype(jnp.bfloat16)
    blocks = blocks.reshape(2, SPIN * OPS, NEV, NEV)
    block_ids = lists_time.reshape(OWNERS, PAIRS, 2).astype(jnp.int32)
    first = blocks[:, block_ids[:, :, 0]].astype(jnp.float32)
    second = blocks[:, block_ids[:, :, 1]].astype(jnp.float32)
    real_sum = jnp.einsum('wpik,wpkj->wij', first[0], second[0]) - jnp.einsum('wpik,wpkj->wij', first[1], second[1])
    imag_sum = jnp.einsum('wpik,wpkj->wij', first[0], second[1]) + jnp.einsum('wpik,wpkj->wij', first[1], second[0])
    normalizer = 1.0 / jnp.sqrt(jnp.float32(2 * NEV * PAIRS))
    return jnp.stack([real_sum, imag_sum]) * normalizer

def reference(perambulator, meson_ops, diagram_lists):
    results = lax.map(one_time, (jnp.moveaxis(perambulator, 1, 0), jnp.moveaxis(meson_ops, 2, 0), diagram_lists))
    return jnp.moveaxis(results, 0, 1)
```

```python
import jax
import jax.numpy as jnp
from jax import lax
from jax.experimental import pallas as pl
from jax.experimental.pallas import tpu as pltpu
from jax.sharding import PartitionSpec as P


def block_step_kernel(slots, ids_ref, me_ref, ops_hbm, *refs):
    count = len(slots)
    peram_refs = refs[: 2 * count]
    out_hbm = refs[2 * count + 1]
    op_buf, weight, result, op_sem, out_sem = refs[2 * count + 2 :]
    half = op_buf.shape[-1]
    ops_count = ops_hbm.shape[1]
    sa_count = 2 * (me_ref.shape[0] * 8)
    me = me_ref[0]
    positions = out_hbm.shape[0]
    for at, (behind, other) in enumerate(slots):
        zpos = lax.rem(me // 2 - behind + sa_count // 2, sa_count // 2)
        core = lax.rem(me + other, 2)
        spin = 2 * zpos + core
        real = peram_refs[2 * at]
        imag = peram_refs[2 * at + 1]
        weight[:half, :half] = real[...]
        weight[:half, half:] = -imag[...]
        weight[half:, :half] = imag[...]
        weight[half:, half:] = real[...]

        def one(q, carry):
            ident = ids_ref[q]

            @pl.when(ident // ops_count == spin)
            def _():
                op = lax.rem(ident, ops_count)
                loads = [
                    pltpu.make_async_copy(ops_hbm.at[part, op], op_buf.at[part], op_sem.at[part])
                    for part in range(2)
                ]
                for load in loads:
                    load.start()
                for load in loads:
                    load.wait()
                left = jnp.concatenate([op_buf[0], op_buf[1]], axis=1)
                product = lax.dot_general(
                    left, weight[...], (((1,), (1,)), ((), ())), preferred_element_type=jnp.float32
                )
                result[0] = product[:, :half].astype(jnp.bfloat16)
                result[1] = product[:, half:].astype(jnp.bfloat16)
                store = pltpu.make_async_copy(result, out_hbm.at[q], out_sem)
                store.start()
                store.wait()

            return carry

        lax.fori_loop(0, positions, one, 0)


def block_step(slots, ids, me, ops, perams, blocks):
    count = len(slots)
    half = ops.shape[-1]
    smem = pl.BlockSpec(memory_space=pltpu.SMEM)
    vmem = pl.BlockSpec(memory_space=pltpu.VMEM)
    hbm = pl.BlockSpec(memory_space=pl.ANY)
    return pl.pallas_call(
        lambda *refs: block_step_kernel(slots, *refs),
        out_shape=jax.ShapeDtypeStruct(blocks.shape, blocks.dtype),
        in_specs=[smem, smem, hbm] + [vmem] * (2 * count) + [hbm],
        out_specs=hbm,
        scratch_shapes=[
            pltpu.VMEM((2, half, half), jnp.bfloat16),
            pltpu.VMEM((2 * half, 2 * half), jnp.bfloat16),
            pltpu.VMEM((2, half, half), jnp.bfloat16),
            pltpu.SemaphoreType.DMA((2,)),
            pltpu.SemaphoreType.DMA,
        ],
        input_output_aliases={3 + 2 * count: 0},
        name="block_step",
    )(ids, me, ops, *perams, blocks)


def pair_kernel(blocks_ref, out_ref, right):
    pair = pl.program_id(0)
    half = out_ref.shape[-1]
    right[:half, :half] = blocks_ref[1, 0]
    right[:half, half:] = blocks_ref[1, 1]
    right[half:, :half] = -blocks_ref[1, 1]
    right[half:, half:] = blocks_ref[1, 0]
    left = jnp.concatenate([blocks_ref[0, 0], blocks_ref[0, 1]], axis=1)
    product = lax.dot_general(
        left, right[...], (((1,), (0,)), ((), ())), preferred_element_type=jnp.float32
    )

    @pl.when(pair == 0)
    def _():
        out_ref[0] = product[:, :half]
        out_ref[1] = product[:, half:]

    @pl.when(pair > 0)
    def _():
        out_ref[0] += product[:, :half]
        out_ref[1] += product[:, half:]

    @pl.when(pair == pl.num_programs(0) - 1)
    def _():
        pairs = pl.num_programs(0)
        scale = 1.0 / jnp.sqrt(jnp.float32(2 * half * 8))
        out_ref[...] = out_ref[...] * scale


def pair_sum(blocks):
    half = blocks.shape[-1]
    pairs = blocks.shape[0] // 2
    return pl.pallas_call(
        pair_kernel,
        out_shape=jax.ShapeDtypeStruct((2, half, half), jnp.float32),
        grid=(pairs,),
        in_specs=[pl.BlockSpec((2, 2, half, half), lambda p: (p, 0, 0, 0))],
        out_specs=pl.BlockSpec((2, half, half), lambda p: (0, 0, 0)),
        scratch_shapes=[pltpu.VMEM((2 * half, 2 * half), jnp.bfloat16)],
        name="pair_sum",
    )(blocks)


def uninitialised(shape, dtype):
    return pl.pallas_call(
        lambda out: None,
        out_shape=jax.ShapeDtypeStruct(shape, dtype),
        out_specs=pl.BlockSpec(memory_space=pl.ANY),
        name="block_room",
    )()


def body(perambulator, meson_ops, diagram_lists):
    eig_count = perambulator.shape[-1]
    sa_count = lax.axis_size("sa")
    ring = sa_count // 2

    def owned(part):
        sent = perambulator[part, :, 0]
        got = lax.all_to_all(sent, "ta", split_axis=0, concat_axis=0, tiled=True)
        return got.reshape(eig_count, eig_count)

    def hop(value, step):
        return lax.ppermute(value, "sa", [(i, (i + 2 * step) % sa_count) for i in range(sa_count)])

    def swap(value):
        return lax.ppermute(value, "sa", [(i, i ^ 1) for i in range(sa_count)])

    ids = diagram_lists.reshape(-1)
    me = lax.axis_index("sa").astype(jnp.int32).reshape(1)
    ops = meson_ops[:, :, 0]
    real, imag = owned(0), owned(1)
    far = ring // 2
    reals = {0: real}
    imags = {0: imag}
    up = down = real
    iup = idown = imag
    for d in range(1, far + 1):
        up = hop(up, 1)
        reals[d] = up
        if d < far:
            down = hop(down, -1)
            reals[ring - d] = down
            iup = hop(iup, 1)
            imags[d] = iup
        idown = hop(idown, -1)
        imags[(ring - d) % ring] = idown
    blocks = uninitialised((ids.shape[0], 2, eig_count, eig_count), jnp.bfloat16)
    for d in range(far + 1):
        where = [d] if d in (0, far) else [d, ring - d]
        slots, perams = [], []
        for behind in where:
            slots += [(behind, 0), (behind, 1)]
            perams += [reals[behind], imags[behind], swap(reals[behind]), swap(imags[behind])]
        blocks = block_step(slots, ids, me, ops, perams, blocks)
    return pair_sum(blocks)[:, None, None]


def solution(mesh):
    in_specs = (
        P(None, None, "sa", "ta", None),
        P(None, None, "ta", None, None),
        P("ta", "sa", None),
    )
    out_specs = P(None, "ta", "sa", None, None)
    return jax.shard_map(body, mesh=mesh, in_specs=in_specs, out_specs=out_specs, check_vma=False)
```

```python
import jax
import jax.numpy as jnp
from jax import lax
from jax.experimental import pallas as pl
from jax.experimental.pallas import tpu as pltpu
from jax.sharding import PartitionSpec as P


MIB = 1 << 20
LIMIT = 16


def dot(left, right, dims):
    return lax.dot_general(left, right, (dims, ((), ())), preferred_element_type=jnp.float32)


def block_step_kernel(slots, ids_ref, me_ref, ops_ref, *refs):
    count = len(slots)
    peram_refs = refs[: 2 * count]
    out_ref, weight = refs[-2:]
    half = ops_ref.shape[-1]
    ops_count = ops_ref.shape[1]
    positions = out_ref.shape[0]
    ring = 8
    me = me_ref[0]
    for at, (behind, other) in enumerate(slots):
        zpos = lax.rem(me // 2 + (ring - behind), ring)
        core = lax.rem(me + other, 2)
        spin = 2 * zpos + core
        real = peram_refs[2 * at]
        imag = peram_refs[2 * at + 1]
        weight[:half, :half] = real[...]
        weight[:half, half:] = -imag[...]
        weight[half:, :half] = imag[...]
        weight[half:, half:] = real[...]

        def one(q, carry):
            ident = ids_ref[q]

            @pl.when(ident // ops_count == spin)
            def _():
                op = lax.rem(ident, ops_count)
                left = jnp.concatenate([ops_ref[0, op], ops_ref[1, op]], axis=1)
                product = dot(left, weight[...], ((1,), (1,)))
                out_ref[q, 0] = product[:, :half].astype(jnp.bfloat16)
                out_ref[q, 1] = product[:, half:].astype(jnp.bfloat16)

            return carry

        lax.fori_loop(0, positions, one, 0)


def block_step(slots, ids, me, ops, perams, blocks):
    count = len(slots)
    half = ops.shape[-1]
    smem = pl.BlockSpec(memory_space=pltpu.SMEM)
    vmem = pl.BlockSpec(memory_space=pltpu.VMEM)
    earlier = [] if blocks is None else [blocks]
    return pl.pallas_call(
        lambda *refs: block_step_kernel(slots, *refs),
        out_shape=jax.ShapeDtypeStruct((ids.shape[0], 2, half, half), jnp.bfloat16),
        in_specs=[smem, smem] + [vmem] * (1 + 2 * count + len(earlier)),
        out_specs=vmem,
        scratch_shapes=[pltpu.VMEM((2 * half, 2 * half), jnp.bfloat16)],
        input_output_aliases={3 + 2 * count: 0} if earlier else {},
        compiler_params=pltpu.CompilerParams(vmem_limit_bytes=LIMIT * MIB),
        cost_estimate=pl.CostEstimate(
            flops=count * 8 * half**3, transcendentals=0, bytes_accessed=count * 4 * half**2
        ),
        name="block_step",
    )(ids, me, ops, *perams, *earlier)


def pair_kernel(blocks_ref, out_ref, right):
    half = out_ref.shape[-1]
    pairs = blocks_ref.shape[0] // 2
    for pair in range(pairs):
        right[:half, :half] = blocks_ref[2 * pair + 1, 0]
        right[:half, half:] = blocks_ref[2 * pair + 1, 1]
        right[half:, :half] = -blocks_ref[2 * pair + 1, 1]
        right[half:, half:] = blocks_ref[2 * pair + 1, 0]
        left = jnp.concatenate([blocks_ref[2 * pair, 0], blocks_ref[2 * pair, 1]], axis=1)
        product = dot(left, right[...], ((1,), (0,)))
        scale = 1.0 / jnp.sqrt(jnp.float32(2 * half * pairs))
        for part in range(2):
            term = product[:, part * half : (part + 1) * half]
            if pair:
                term = out_ref[part] + term
            if pair == pairs - 1:
                term = term * scale
            out_ref[part] = term


def pair_sum(blocks):
    half = blocks.shape[-1]
    vmem = pl.BlockSpec(memory_space=pltpu.VMEM)
    return pl.pallas_call(
        pair_kernel,
        out_shape=jax.ShapeDtypeStruct((2, half, half), jnp.float32),
        in_specs=[vmem],
        out_specs=vmem,
        scratch_shapes=[pltpu.VMEM((2 * half, 2 * half), jnp.bfloat16)],
        compiler_params=pltpu.CompilerParams(vmem_limit_bytes=LIMIT * MIB),
        name="pair_sum",
    )(blocks)


def placed(perambulator, meson_ops, diagram_lists):
    sa_count = lax.axis_size("sa")
    ring = sa_count // 2
    far = ring // 2

    def hop(value, step):
        return lax.ppermute(value, "sa", [(i, (i + 2 * step) % sa_count) for i in range(sa_count)])

    def swap(value):
        return lax.ppermute(value, "sa", [(i, i ^ 1) for i in range(sa_count)])

    ids = diagram_lists.reshape(-1)
    me = lax.axis_index("sa").astype(jnp.int32).reshape(1)
    ops = meson_ops[:, :, 0]
    owned = lax.all_to_all(perambulator, "ta", split_axis=1, concat_axis=3, tiled=True)
    real, imag = owned[0, 0, 0], owned[1, 0, 0]
    reals, imags = {0: real}, {0: imag}
    up = down = real
    iup = idown = imag
    for d in range(1, far + 1):
        up = hop(up, 1)
        reals[d] = up
        if d < far:
            down = hop(down, -1)
            reals[ring - d] = down
            iup = hop(iup, 1)
            imags[d] = iup
        idown = hop(idown, -1)
        imags[(ring - d) % ring] = idown
    blocks = None
    for d in range(far + 1):
        where = [d] if d in (0, far) else [d, ring - d]
        slots, perams = [], []
        for behind in where:
            slots += [(behind, 0), (behind, 1)]
            perams += [reals[behind], imags[behind], swap(reals[behind]), swap(imags[behind])]
        blocks = block_step(slots, ids, me, ops, perams, blocks)
    return pair_sum(blocks)[:, None, None]


def solution(mesh):
    in_specs = (
        P(None, None, "sa", "ta", None),
        P(None, None, "ta", None, None),
        P("ta", "sa", None),
    )
    out_specs = P(None, "ta", "sa", None, None)
    return jax.shard_map(placed, mesh=mesh, in_specs=in_specs, out_specs=out_specs, check_vma=False)
```

```python
import jax
import jax.numpy as jnp
from jax import lax
from jax.experimental import pallas as pl
from jax.experimental.pallas import tpu as pltpu
from jax.sharding import PartitionSpec as P

LIMIT = 16 << 20
ROOM = (5, 10, 10, 8)
OPERATOR, FIRST, LAST, USES, WHEN, TABLE = 0, 16, 32, 48, 64, 128


def dot(left, right, dims):
    return lax.dot_general(left, right, (dims, ((), ())), preferred_element_type=jnp.float32)


def fill_table(table, ids_ref, me, ring, ops_count, positions):
    for slot in range(2 * ring):
        table[USES + slot] = 0
    arrival = []
    load = [jnp.int32(0) for _ in range(ring // 2 + 1)]
    for q in range(positions):
        ident = ids_ref[q]
        spin = lax.div(ident, ops_count)
        table[OPERATOR + q] = ident - spin * ops_count
        behind = jnp.bitwise_and((me >> 1) - (spin >> 1), ring - 1)
        slot = 2 * behind + jnp.bitwise_xor(jnp.bitwise_and(me, 1), jnp.bitwise_and(spin, 1))
        count = table[USES + slot]
        table[FIRST + slot] = jnp.where(count == 0, q, table[FIRST + slot])
        table[LAST + slot] = q
        table[USES + slot] = count + 1
        step = jnp.minimum(behind, ring - behind)
        arrival.append(step)
        load = [n + jnp.where(step == d, 1, 0) for d, n in enumerate(load)]
    final = ring // 2
    when = [jnp.int32(final) for _ in range(positions // 2)]
    for d in range(final):
        for p in range(positions // 2):
            ready = jnp.maximum(arrival[2 * p], arrival[2 * p + 1])
            take = (when[p] == final) & (ready <= d) & (load[d] < ROOM[d])
            when[p] = jnp.where(take, d, when[p])
            load[d] = load[d] + jnp.where(take, 1, 0)
    for p in range(positions // 2):
        table[WHEN + p] = when[p]


def make_blocks(slot, real, imag, table, ops_ref, left_ref, right_ref, weight):
    half = ops_ref.shape[-1]
    uses = table[USES + slot]

    @pl.when(uses > 0)
    def _():
        weight[:half, :half] = real[...]
        weight[:half, half:] = -imag[...]
        weight[half:, :half] = imag[...]
        weight[half:, half:] = real[...]

        def one(use, carry):
            q = jnp.where(use == 0, table[FIRST + slot], table[LAST + slot])
            op = table[OPERATOR + q]
            stacked = jnp.concatenate([ops_ref[0, op], ops_ref[1, op]], axis=1)
            block = dot(stacked, weight[...], ((1,), (1,))).astype(jnp.bfloat16)
            p = q >> 1

            @pl.when(jnp.bitwise_and(q, 1) == 0)
            def _():
                left_ref[p] = block

            @pl.when(jnp.bitwise_and(q, 1) == 1)
            def _():
                right_ref[p, :half] = block
                right_ref[p, half:, :half] = -block[:, half:]
                right_ref[p, half:, half:] = block[:, :half]

            return carry

        lax.fori_loop(0, uses, one, 0)


def add_pairs(step, table, left_ref, right_ref, sum_ref):
    half = sum_ref.shape[-1]

    def pair(p, carry):
        @pl.when(table[WHEN + p] == step)
        def _():
            product = dot(left_ref[p], right_ref[p], ((1,), (0,)))
            sum_ref[0] += product[:, :half]
            sum_ref[1] += product[:, half:]

        return carry

    lax.fori_loop(0, left_ref.shape[0], pair, 0)


def work(slots, parts, inputs, ops, step=None, final=False, ids=None, me=None, ring=None):
    half = ops.shape[-1]
    smem = pl.BlockSpec(memory_space=pltpu.SMEM)
    vmem = pl.BlockSpec(memory_space=pltpu.VMEM)
    arrays = [array for pair in parts for array in pair[:1 if pair[1] is None else 2]]
    starts = ids is not None
    table, left, right, total = inputs
    pairs = 8 if starts else left.shape[0]
    blocks_shape = (
        jax.ShapeDtypeStruct((pairs, half, 2 * half), jnp.bfloat16),
        jax.ShapeDtypeStruct((pairs, 2 * half, 2 * half), jnp.bfloat16),
    )
    sum_shape = jax.ShapeDtypeStruct((2, half, half), jnp.float32)
    scratch = [pltpu.VMEM((2 * half, 2 * half), jnp.bfloat16)]
    out_shape, out_specs, aliases = [], [], {}
    operands = [ids, me] if starts else [table]
    in_specs = [smem] * len(operands)
    operands += [ops, *arrays]
    if starts:
        out_shape += [jax.ShapeDtypeStruct((TABLE,), jnp.int32), *blocks_shape]
        out_specs += [smem, vmem, vmem]
    else:
        kept = [left, right]
        aliases = {len(operands): 0, len(operands) + 1: 1}
        out_shape += blocks_shape
        out_specs += [vmem, vmem]
        if step is not None:
            if total is not None:
                kept.append(total)
                if not final:
                    aliases[len(operands) + 2] = len(out_shape)
            out_shape.append(sum_shape)
            out_specs.append(vmem)
        operands += kept
    in_specs += [vmem] * (len(operands) - len(in_specs))

    def kernel(*refs):
        given, outs, weight = refs[: len(operands)], refs[len(operands) : -1], refs[-1]
        if starts:
            ids_ref, me_ref, ops_ref = given[:3]
            at = 3
            table_ref, left_ref, right_ref = outs
            fill_table(table_ref, ids_ref, me_ref[0], ring, ops_ref.shape[1], ids_ref.shape[0])
        else:
            table_ref, ops_ref = given[:2]
            at = 2
            left_ref, right_ref = outs[:2]
        for slot, pair in zip(slots, parts, strict=True):
            if pair[1] is None:
                real, imag = given[at].at[0], given[at].at[1]
                at += 1
            else:
                real, imag = given[at], given[at + 1]
                at += 2
            make_blocks(slot, real, imag, table_ref, ops_ref, left_ref, right_ref, weight)
        if step is None:
            return
        sum_ref = outs[-1]
        if total is None:
            sum_ref[...] = jnp.zeros(sum_ref.shape, jnp.float32)
        elif final:
            sum_ref[...] = given[-1][...]
        add_pairs(step, table_ref, left_ref, right_ref, sum_ref)
        if final:
            sum_ref[...] = sum_ref[...] * (1.0 / jnp.sqrt(jnp.float32(2 * half * pairs)))

    outs = pl.pallas_call(
        kernel,
        out_shape=tuple(out_shape),
        in_specs=in_specs,
        out_specs=tuple(out_specs),
        scratch_shapes=scratch,
        input_output_aliases=aliases,
        compiler_params=pltpu.CompilerParams(vmem_limit_bytes=LIMIT),
        cost_estimate=pl.CostEstimate(
            flops=len(slots) * 8 * half**3, transcendentals=0, bytes_accessed=len(slots) * 4 * half**2
        ),
        name="work",
    )(*operands)
    if starts:
        return (*outs, None)
    if final:
        return outs[2]
    return (table, outs[0], outs[1], outs[2] if step is not None else total)


def placed(perambulator, meson_ops, diagram_lists):
    sa_count = lax.axis_size("sa")
    ring = sa_count // 2
    far = ring // 2

    def hop(value, step):
        return lax.ppermute(value, "sa", [(i, (i + 2 * step) % sa_count) for i in range(sa_count)])

    def swap(value):
        return lax.ppermute(value, "sa", [(i, i ^ 1) for i in range(sa_count)])

    ids = diagram_lists.reshape(-1)
    me = lax.axis_index("sa").astype(jnp.int32).reshape(1)
    ops = meson_ops[:, :, 0]
    owned = lax.all_to_all(perambulator, "ta", split_axis=1, concat_axis=3, tiled=True)[:, 0, 0]
    up = {0: owned}
    down = {0: owned}
    for d in range(1, far):
        up[d] = hop(up[d - 1], 1)
        down[d] = hop(down[d - 1], -1)
    up[far] = hop(up[far - 1][0], 1)
    down[far] = hop(down[far - 1][1], -1)
    state = (None, None, None, None)
    for d in range(far + 1):
        other_up = swap(up[d])
        other_down = swap(down[d]) if d else None
        if d == far:
            own, other = [(up[d], down[d])], [(other_up, other_down)]
            slots = [2 * d]
        elif d:
            own, other = [(up[d], None), (down[d], None)], [(other_up, None), (other_down, None)]
            slots = [2 * d, 2 * (ring - d)]
        else:
            own, other = [(up[d], None)], [(other_up, None)]
            slots = [0]
        begin = {} if d else {"ids": ids, "me": me, "ring": ring}
        state = work(slots, own, state, ops, **begin)
        state = work([s + 1 for s in slots], other, state, ops, step=d, final=d == far)
    return state[:, None, None]


def solution(mesh):
    in_specs = (
        P(None, None, "sa", "ta", None),
        P(None, None, "ta", None, None),
        P("ta", "sa", None),
    )
    out_specs = P(None, "ta", "sa", None, None)
    return jax.shard_map(placed, mesh=mesh, in_specs=in_specs, out_specs=out_specs, check_vma=False)
```

```python
import jax
import jax.numpy as jnp
from jax import lax
from jax.experimental import pallas as pl
from jax.experimental.pallas import tpu as pltpu
from jax.sharding import PartitionSpec as P

LIMIT = 16 << 20
OPERATOR, FIRST, LAST, USES, KIND, WHEN, TAKE, TABLE = 0, 16, 32, 48, 64, 80, 88, 128
LEFT, RIGHT, LATE = 0, 1, 2


def dot(left, right, dims):
    return lax.dot_general(left, right, (dims, ((), ())), preferred_element_type=jnp.float32)


def fill_table(table, ids_ref, me, ring, ops_count, positions):
    for slot in range(2 * ring):
        table[USES + slot] = 0
    arrival = []
    for q in range(positions):
        ident = ids_ref[q]
        spin = lax.div(ident, ops_count)
        table[OPERATOR + q] = ident - spin * ops_count
        behind = jnp.bitwise_and((me >> 1) - (spin >> 1), ring - 1)
        slot = 2 * behind + jnp.bitwise_xor(jnp.bitwise_and(me, 1), jnp.bitwise_and(spin, 1))
        count = table[USES + slot]
        table[FIRST + slot] = jnp.where(count == 0, q, table[FIRST + slot])
        table[LAST + slot] = q
        table[USES + slot] = count + 1
        arrival.append(jnp.minimum(behind, ring - behind))
    for p in range(positions // 2):
        left_at, right_at = arrival[2 * p], arrival[2 * p + 1]
        late = right_at > left_at
        table[KIND + 2 * p] = LEFT
        table[KIND + 2 * p + 1] = jnp.where(late, LATE, RIGHT)
        table[TAKE + p] = jnp.where(late, left_at, -1)
        table[WHEN + p] = jnp.where(late, -1, left_at)


def place_weights(parts, weight):
    half = weight.shape[-1] // 2
    for n, (real, imag) in enumerate(parts):
        weight[n, :half, :half] = real[...]
        weight[n, :half, half:] = -imag[...]
        weight[n, half:, :half] = imag[...]
        weight[n, half:, half:] = real[...]


def make_blocks(slots, table, ops_ref, left_ref, right_ref, sum_ref, weight, late_too):
    half = ops_ref.shape[-1]

    def one(at, carry):
        n = at >> 1
        use = jnp.bitwise_and(at, 1)
        slot = jnp.int32(slots[0])
        for other, value in enumerate(slots[1:], 1):
            slot = jnp.where(n == other, value, slot)

        @pl.when(use < table[USES + slot])
        def _():
            q = jnp.where(use == 0, table[FIRST + slot], table[LAST + slot])
            kind = table[KIND + q]
            p = q >> 1

            @pl.when(kind != LATE)
            def _():
                op = table[OPERATOR + q]
                stacked = jnp.concatenate([ops_ref[0, op], ops_ref[1, op]], axis=1)
                block = dot(stacked, weight[n], ((1,), (1,))).astype(jnp.bfloat16)

                @pl.when(kind == LEFT)
                def _():
                    left_ref[p] = block

                @pl.when(kind == RIGHT)
                def _():
                    right_ref[p, :half] = block
                    right_ref[p, half:, :half] = -block[:, half:]
                    right_ref[p, half:, half:] = block[:, :half]

            if late_too:

                @pl.when(kind == LATE)
                def _():
                    product = dot(left_ref[p], weight[n], ((1,), (1,)))
                    sum_ref[0] += product[:, :half]
                    sum_ref[1] += product[:, half:]

        return carry

    lax.fori_loop(0, 2 * len(slots), one, 0)


def take_operators(step, table, ops_ref, left_ref, weight):
    half = ops_ref.shape[-1]

    def pair(p, carry):
        @pl.when(table[TAKE + p] == step)
        def _():
            op = table[OPERATOR + 2 * p + 1]
            weight[0, :half, :half] = ops_ref[0, op]
            weight[0, :half, half:] = ops_ref[1, op]
            weight[0, half:, :half] = -ops_ref[1, op]
            weight[0, half:, half:] = ops_ref[0, op]
            left_ref[p] = dot(left_ref[p], weight[0], ((1,), (0,))).astype(jnp.bfloat16)

        return carry

    lax.fori_loop(0, left_ref.shape[0], pair, 0)


def add_pairs(step, table, left_ref, right_ref, sum_ref, rows):
    half = sum_ref.shape[-1]

    def pair(p, carry):
        @pl.when(table[WHEN + p] == step)
        def _():
            product = dot(left_ref[p, rows], right_ref[p], ((1,), (0,)))
            sum_ref[0, rows] += product[:, :half]
            sum_ref[1, rows] += product[:, half:]

        return carry

    lax.fori_loop(0, left_ref.shape[0], pair, 0)


def work(slots, parts, state, ops, step=None, final=False, begin=None):
    half = ops.shape[-1]
    smem = pl.BlockSpec(memory_space=pltpu.SMEM)
    vmem = pl.BlockSpec(memory_space=pltpu.VMEM)
    arrays = [array for pair in parts for array in pair if array is not None]
    if begin:
        ids, me, ring = begin
        pairs = ids.shape[0] // 2
        operands, in_specs = [ids, me, ops, *arrays], [smem, smem]
        out_shape = [jax.ShapeDtypeStruct((TABLE,), jnp.int32)]
        out_specs, aliases = [smem, vmem, vmem, vmem], {}
    else:
        pairs = state[1].shape[0]
        operands, in_specs = [state[0], ops, *arrays, *state[1:]], []
        out_shape, out_specs = [], [vmem, vmem, vmem]
        aliases = {2 + len(arrays) + n: n for n in range(3)}
    in_specs += [vmem] * (len(operands) - len(in_specs))
    out_shape += [
        jax.ShapeDtypeStruct((pairs, half, 2 * half), jnp.bfloat16),
        jax.ShapeDtypeStruct((pairs, 2 * half, 2 * half), jnp.bfloat16),
        jax.ShapeDtypeStruct((2, half, half), jnp.float32),
    ]
    scratch = [pltpu.VMEM((len(slots), 2 * half, 2 * half), jnp.bfloat16)]
    chunks = 3
    if not begin:
        scratch += [pltpu.SMEM((TABLE,), jnp.int32), pltpu.SemaphoreType.DMA]
    if final:
        out_shape.append(jax.ShapeDtypeStruct((2, half, half), jnp.float32))
        out_specs.append(pl.BlockSpec(memory_space=pl.ANY))
        scratch.append(pltpu.SemaphoreType.DMA((chunks,)))

    def kernel(*refs):
        given = refs[: len(operands)]
        outs = refs[len(operands) : len(operands) + len(out_shape)]
        weight = refs[len(operands) + len(out_shape)]
        if begin:
            ids_ref, me_ref, ops_ref = given[:3]
            at = 3
            table, left_ref, right_ref, sum_ref = outs
            fill_table(table, ids_ref, me_ref[0], ring, ops_ref.shape[1], ids_ref.shape[0])
            sum_ref[...] = jnp.zeros(sum_ref.shape, jnp.float32)
        else:
            ops_ref = given[1]
            at = 2
            table = refs[len(operands) + len(out_shape) + 1]
            fetch = pltpu.make_async_copy(given[0], table, refs[len(operands) + len(out_shape) + 2])
            fetch.start()
            left_ref, right_ref, sum_ref = outs[:3]
        sources = []
        for pair in parts:
            if pair[1] is None:
                sources.append((given[at].at[0], given[at].at[1]))
                at += 1
            else:
                sources.append((given[at], given[at + 1]))
                at += 2
        place_weights(sources, weight)
        if not begin:
            fetch.wait()
        make_blocks(slots, table, ops_ref, left_ref, right_ref, sum_ref, weight, slots[0] > 1)
        if step is None:
            return
        if not final:
            take_operators(step, table, ops_ref, left_ref, weight)
            add_pairs(step, table, left_ref, right_ref, sum_ref, slice(None))
            return
        copies = []
        for n in range(chunks):
            rows = slice(n * half // chunks, (n + 1) * half // chunks)
            add_pairs(step, table, left_ref, right_ref, sum_ref, rows)
            scale = 1.0 / jnp.sqrt(jnp.float32(2 * half * pairs))
            sum_ref[:, rows] = sum_ref[:, rows] * scale
            copies.append(
                pltpu.make_async_copy(
                    sum_ref.at[:, rows], outs[3].at[:, rows], refs[-1].at[n]
                )
            )
            copies[-1].start()
        for copy in copies:
            copy.wait()

    outs = pl.pallas_call(
        kernel,
        out_shape=tuple(out_shape),
        in_specs=in_specs,
        out_specs=tuple(out_specs),
        scratch_shapes=scratch,
        input_output_aliases=aliases,
        compiler_params=pltpu.CompilerParams(vmem_limit_bytes=LIMIT),
        cost_estimate=pl.CostEstimate(
            flops=len(slots) * 8 * half**3, transcendentals=0, bytes_accessed=len(slots) * 4 * half**2
        ),
        name="work",
    )(*operands)
    if final:
        return outs[3]
    return tuple(outs) if begin else (state[0], *outs)


def placed(perambulator, meson_ops, diagram_lists):
    sa_count = lax.axis_size("sa")
    ring = sa_count // 2
    far = ring // 2

    def hop(value, step):
        return lax.ppermute(value, "sa", [(i, (i + 2 * step) % sa_count) for i in range(sa_count)])

    def swap(value):
        return lax.ppermute(value, "sa", [(i, i ^ 1) for i in range(sa_count)])

    ids = diagram_lists.reshape(-1)
    me = lax.axis_index("sa").astype(jnp.int32).reshape(1)
    ops = meson_ops[:, :, 0]
    owned = lax.all_to_all(perambulator, "ta", split_axis=1, concat_axis=3, tiled=True)[:, 0, 0]
    up = {0: owned}
    down = {0: owned}
    for d in range(1, far):
        up[d] = hop(up[d - 1], 1)
        down[d] = hop(down[d - 1], -1)
    up[far] = hop(up[far - 1][0], 1)
    down[far] = hop(down[far - 1][1], -1)
    state = None
    for d in range(far + 1):
        other_up = swap(up[d])
        other_down = swap(down[d]) if d else None
        if d == far:
            own, other = [(up[d], down[d])], [(other_up, other_down)]
            slots = [2 * d]
        elif d:
            own, other = [(up[d], None), (down[d], None)], [(other_up, None), (other_down, None)]
            slots = [2 * d, 2 * (ring - d)]
        else:
            own, other = [(up[d], None)], [(other_up, None)]
            slots = [0]
        state = work(slots, own, state, ops, begin=None if d else (ids, me, ring))
        state = work([s + 1 for s in slots], other, state, ops, step=d, final=d == far)
    return state[:, None, None]


def solution(mesh):
    in_specs = (
        P(None, None, "sa", "ta", None),
        P(None, None, "ta", None, None),
        P("ta", "sa", None),
    )
    out_specs = P(None, "ta", "sa", None, None)
    return jax.shard_map(placed, mesh=mesh, in_specs=in_specs, out_specs=out_specs, check_vma=False)
```

```python
import jax
import jax.numpy as jnp
from jax import lax
from jax.experimental import pallas as pl
from jax.experimental.pallas import tpu as pltpu
from jax.sharding import PartitionSpec as P

LIMIT = 16 << 20
FIRST, LAST, USES, SCALARS = 0, 16, 32, 128
WHEN, TAKE, OPERATORS = 16, 24, 32
LEFT, RIGHT, LATE = 0, 1, 2
ROW, LANES = 8, 128


def dot(left, right, dims):
    return lax.dot_general(left, right, (dims, ((), ())), preferred_element_type=jnp.float32)


def fill_table(table, scalars, ids_ref, me, ring, ops_count, positions):
    for slot in range(2 * ring):
        scalars[FIRST + slot] = 0
        scalars[LAST + slot] = 0
        scalars[USES + slot] = 0
    arrival, operators = [], []
    for q in range(positions):
        ident = ids_ref[q]
        spin = lax.div(ident, ops_count)
        operators.append(ident - spin * ops_count)
        behind = jnp.bitwise_and((me >> 1) - (spin >> 1), ring - 1)
        slot = 2 * behind + jnp.bitwise_xor(jnp.bitwise_and(me, 1), jnp.bitwise_and(spin, 1))
        arrival.append(jnp.minimum(behind, ring - behind))
        count = scalars[USES + slot]
        scalars[USES + slot] = count + 1
        scalars[FIRST + slot] = jnp.where(count == 0, q, scalars[FIRST + slot])
        scalars[LAST + slot] = q
    steps = ring // 2 + 1
    when, take = [jnp.int32(0)] * steps, [jnp.int32(0)] * steps
    taken = jnp.int32(0)
    for p in range(positions // 2):
        left_at, right_at = arrival[2 * p], arrival[2 * p + 1]
        late = right_at > left_at
        entry = p * 8 + operators[2 * p]
        scalars[48 + 2 * p] = LEFT * 64 + entry
        entry = p * 8 + operators[2 * p + 1]
        scalars[48 + 2 * p + 1] = jnp.where(late, LATE * 64, RIGHT * 64) + entry
        taken = taken + (operators[2 * p + 1] << (3 * p))
        for d in range(steps):
            at = left_at == d
            when[d] = when[d] + jnp.where(at & jnp.logical_not(late), 1 << p, 0)
            take[d] = take[d] + jnp.where(at & late, 1 << p, 0)
    lane = lax.broadcasted_iota(jnp.int32, (ROW, LANES), 1)
    row = jnp.zeros((ROW, LANES), jnp.int32)
    for slot in range(2 * ring):
        one = scalars[48 + scalars[FIRST + slot]]
        two = scalars[48 + scalars[LAST + slot]]
        packed = scalars[USES + slot] + (one << 2) + (two << 10)
        row = jnp.where(lane == slot, packed, row)
    for d in range(steps):
        row = jnp.where(lane == WHEN + d, when[d], row)
        row = jnp.where(lane == TAKE + d, take[d], row)
    table[...] = jnp.where(lane == OPERATORS, taken, row)


def place_weights(parts, weight):
    half = weight.shape[-1] // 2
    for n, (real, imag) in enumerate(parts):
        weight[n, :half, :half] = real[...]
        weight[n, :half, half:] = -imag[...]
        weight[n, half:, :half] = imag[...]
        weight[n, half:, half:] = real[...]


def make_blocks(entries, ops_ref, left_ref, right_ref, sum_ref, weight, late_too):
    half = ops_ref.shape[-1]

    def one(at, carry):
        n = at >> 1
        use = jnp.bitwise_and(at, 1)
        packed = entries[0]
        for other, value in enumerate(entries[1:], 1):
            packed = jnp.where(n == other, value, packed)

        @pl.when(use < jnp.bitwise_and(packed, 3))
        def _():
            entry = jnp.bitwise_and(jnp.where(use == 0, packed >> 2, packed >> 10), 255)
            kind = entry >> 6
            p = jnp.bitwise_and(entry >> 3, 7)

            @pl.when(kind != LATE)
            def _():
                op = jnp.bitwise_and(entry, 7)
                stacked = jnp.concatenate([ops_ref[0, op], ops_ref[1, op]], axis=1)
                block = dot(stacked, weight[n], ((1,), (1,))).astype(jnp.bfloat16)

                @pl.when(kind == LEFT)
                def _():
                    left_ref[p] = block

                @pl.when(kind == RIGHT)
                def _():
                    right_ref[p, :half] = block
                    right_ref[p, half:, :half] = -block[:, half:]
                    right_ref[p, half:, half:] = block[:, :half]

            if late_too:

                @pl.when(kind == LATE)
                def _():
                    product = dot(left_ref[p], weight[n], ((1,), (1,)))
                    sum_ref[0] += product[:, :half]
                    sum_ref[1] += product[:, half:]

        return carry

    lax.fori_loop(0, 2 * len(entries), one, 0)


def take_operators(mask, operators, ops_ref, left_ref, weight):
    half = ops_ref.shape[-1]

    def pair(p, carry):
        @pl.when(jnp.bitwise_and(mask >> p, 1) == 1)
        def _():
            op = jnp.bitwise_and(operators >> (3 * p), 7)
            weight[0, :half, :half] = ops_ref[0, op]
            weight[0, :half, half:] = ops_ref[1, op]
            weight[0, half:, :half] = -ops_ref[1, op]
            weight[0, half:, half:] = ops_ref[0, op]
            left_ref[p] = dot(left_ref[p], weight[0], ((1,), (0,))).astype(jnp.bfloat16)

        return carry

    @pl.when(mask > 0)
    def _():
        lax.fori_loop(0, left_ref.shape[0], pair, 0)


def add_pairs(mask, left_ref, right_ref, sum_ref, rows):
    half = sum_ref.shape[-1]

    def pair(p, carry):
        @pl.when(jnp.bitwise_and(mask >> p, 1) == 1)
        def _():
            product = dot(left_ref[p, rows], right_ref[p], ((1,), (0,)))
            sum_ref[0, rows] += product[:, :half]
            sum_ref[1, rows] += product[:, half:]

        return carry

    @pl.when(mask > 0)
    def _():
        lax.fori_loop(0, left_ref.shape[0], pair, 0)


def work(slots, parts, state, ops, step=None, final=False, begin=None):
    half = ops.shape[-1]
    smem = pl.BlockSpec(memory_space=pltpu.SMEM)
    vmem = pl.BlockSpec(memory_space=pltpu.VMEM)
    arrays = [array for pair in parts for array in pair if array is not None]
    if begin:
        ids, me, ring = begin
        pairs = ids.shape[0] // 2
        operands, in_specs = [ids, me, ops, *arrays], [smem, smem]
        out_shape = [jax.ShapeDtypeStruct((ROW, LANES), jnp.int32)]
        out_specs, aliases = [vmem, vmem, vmem, vmem], {}
    else:
        pairs = state[1].shape[0]
        operands, in_specs = [state[0], ops, *arrays, *state[1:]], []
        out_shape, out_specs = [], [vmem, vmem, vmem]
        aliases = {2 + len(arrays) + n: n for n in range(3)}
    in_specs += [vmem] * (len(operands) - len(in_specs))
    out_shape += [
        jax.ShapeDtypeStruct((pairs, half, 2 * half), jnp.bfloat16),
        jax.ShapeDtypeStruct((pairs, 2 * half, 2 * half), jnp.bfloat16),
        jax.ShapeDtypeStruct((2, half, half), jnp.float32),
    ]
    scratch = [pltpu.VMEM((len(slots), 2 * half, 2 * half), jnp.bfloat16)]
    chunks = 3
    if begin:
        scratch.append(pltpu.SMEM((SCALARS,), jnp.int32))
    if final:
        out_shape.append(jax.ShapeDtypeStruct((2, half, half), jnp.float32))
        out_specs.append(pl.BlockSpec(memory_space=pl.ANY))
        scratch.append(pltpu.SemaphoreType.DMA((chunks,)))

    def kernel(*refs):
        given = refs[: len(operands)]
        outs = refs[len(operands) : len(operands) + len(out_shape)]
        weight = refs[len(operands) + len(out_shape)]
        if begin:
            ids_ref, me_ref, ops_ref = given[:3]
            at = 3
            table, left_ref, right_ref, sum_ref = outs
            fill_table(table, refs[-1], ids_ref, me_ref[0], ring, ops_ref.shape[1], ids_ref.shape[0])
            sum_ref[...] = jnp.zeros(sum_ref.shape, jnp.float32)
        else:
            ops_ref = given[1]
            at = 2
            table = given[0]
            left_ref, right_ref, sum_ref = outs[:3]
        sources = []
        for pair in parts:
            if pair[1] is None:
                sources.append((given[at].at[0], given[at].at[1]))
                at += 1
            else:
                sources.append((given[at], given[at + 1]))
                at += 2
        row = table[...]
        entries = [row[0, slot] for slot in slots]
        if step is not None:
            when = row[0, WHEN + step]
            if not final:
                take, operators = row[0, TAKE + step], row[0, OPERATORS]
        place_weights(sources, weight)
        make_blocks(entries, ops_ref, left_ref, right_ref, sum_ref, weight, slots[0] > 1)
        if step is None:
            return
        if not final:
            take_operators(take, operators, ops_ref, left_ref, weight)
            add_pairs(when, left_ref, right_ref, sum_ref, slice(None))
            return
        copies = []
        for n in range(chunks):
            rows = slice(n * half // chunks, (n + 1) * half // chunks)
            add_pairs(when, left_ref, right_ref, sum_ref, rows)
            scale = 1.0 / jnp.sqrt(jnp.float32(2 * half * pairs))
            sum_ref[:, rows] = sum_ref[:, rows] * scale
            copies.append(
                pltpu.make_async_copy(
                    sum_ref.at[:, rows], outs[3].at[:, rows], refs[-1].at[n]
                )
            )
            copies[-1].start()
        for copy in copies:
            copy.wait()

    outs = pl.pallas_call(
        kernel,
        out_shape=tuple(out_shape),
        in_specs=in_specs,
        out_specs=tuple(out_specs),
        scratch_shapes=scratch,
        input_output_aliases=aliases,
        compiler_params=pltpu.CompilerParams(vmem_limit_bytes=LIMIT),
        cost_estimate=pl.CostEstimate(
            flops=len(slots) * 8 * half**3, transcendentals=0, bytes_accessed=len(slots) * 4 * half**2
        ),
        name="work",
    )(*operands)
    if final:
        return outs[3]
    return tuple(outs) if begin else (state[0], *outs)


def placed(perambulator, meson_ops, diagram_lists):
    sa_count = lax.axis_size("sa")
    ring = sa_count // 2
    far = ring // 2

    def hop(value, step):
        return lax.ppermute(value, "sa", [(i, (i + 2 * step) % sa_count) for i in range(sa_count)])

    def swap(value):
        return lax.ppermute(value, "sa", [(i, i ^ 1) for i in range(sa_count)])

    ids = diagram_lists.reshape(-1)
    me = lax.axis_index("sa").astype(jnp.int32).reshape(1)
    ops = meson_ops[:, :, 0]
    owned = lax.all_to_all(perambulator, "ta", split_axis=1, concat_axis=3, tiled=True)[:, 0, 0]
    up = {0: owned}
    down = {0: owned}
    for d in range(1, far):
        up[d] = hop(up[d - 1], 1)
        down[d] = hop(down[d - 1], -1)
    up[far] = hop(up[far - 1][0], 1)
    down[far] = hop(down[far - 1][1], -1)
    state = None
    for d in range(far + 1):
        other_up = swap(up[d])
        other_down = swap(down[d]) if d else None
        if d == far:
            own, other = [(up[d], down[d])], [(other_up, other_down)]
            slots = [2 * d]
        elif d:
            own, other = [(up[d], None), (down[d], None)], [(other_up, None), (other_down, None)]
            slots = [2 * d, 2 * (ring - d)]
        else:
            own, other = [(up[d], None)], [(other_up, None)]
            slots = [0]
        state = work(slots, own, state, ops, begin=None if d else (ids, me, ring))
        state = work([s + 1 for s in slots], other, state, ops, step=d, final=d == far)
    return state[:, None, None]


def solution(mesh):
    in_specs = (
        P(None, None, "sa", "ta", None),
        P(None, None, "ta", None, None),
        P("ta", "sa", None),
    )
    out_specs = P(None, "ta", "sa", None, None)
    return jax.shard_map(placed, mesh=mesh, in_specs=in_specs, out_specs=out_specs, check_vma=False)
```

```python
import jax
import jax.numpy as jnp
from jax import lax
from jax.experimental import pallas as pl
from jax.experimental.pallas import tpu as pltpu
from jax.sharding import PartitionSpec as P

LIMIT = 16 << 20
FIRST, LAST, USES, SCALARS = 0, 16, 32, 128
WHEN, TAKE, OPERATORS = 16, 24, 32
LEFT, RIGHT, LATE = 0, 1, 2
ROW, LANES = 8, 128


def dot(left, right, dims):
    return lax.dot_general(left, right, (dims, ((), ())), preferred_element_type=jnp.float32)


def fill_table(table, scalars, ids_ref, me, ring, ops_count, positions):
    for slot in range(2 * ring):
        scalars[FIRST + slot] = 0
        scalars[LAST + slot] = 0
        scalars[USES + slot] = 0
    arrival, operators = [], []
    for q in range(positions):
        ident = ids_ref[q]
        spin = lax.div(ident, ops_count)
        operators.append(ident - spin * ops_count)
        behind = jnp.bitwise_and((me >> 1) - (spin >> 1), ring - 1)
        slot = 2 * behind + jnp.bitwise_xor(jnp.bitwise_and(me, 1), jnp.bitwise_and(spin, 1))
        arrival.append(jnp.minimum(behind, ring - behind))
        count = scalars[USES + slot]
        scalars[USES + slot] = count + 1
        scalars[FIRST + slot] = jnp.where(count == 0, q, scalars[FIRST + slot])
        scalars[LAST + slot] = q
    steps = ring // 2 + 1
    when, take = [jnp.int32(0)] * steps, [jnp.int32(0)] * steps
    taken = jnp.int32(0)
    for p in range(positions // 2):
        left_at, right_at = arrival[2 * p], arrival[2 * p + 1]
        late = right_at > left_at
        entry = p * 8 + operators[2 * p]
        scalars[48 + 2 * p] = LEFT * 64 + entry
        entry = p * 8 + operators[2 * p + 1]
        scalars[48 + 2 * p + 1] = jnp.where(late, LATE * 64, RIGHT * 64) + entry
        taken = taken + (operators[2 * p + 1] << (3 * p))
        for d in range(steps):
            at = left_at == d
            when[d] = when[d] + jnp.where(at & jnp.logical_not(late), 1 << p, 0)
            take[d] = take[d] + jnp.where(at & late, 1 << p, 0)
    lane = lax.broadcasted_iota(jnp.int32, (ROW, LANES), 1)
    row = jnp.zeros((ROW, LANES), jnp.int32)
    for slot in range(2 * ring):
        one = scalars[48 + scalars[FIRST + slot]]
        two = scalars[48 + scalars[LAST + slot]]
        packed = scalars[USES + slot] + (one << 2) + (two << 10)
        row = jnp.where(lane == slot, packed, row)
    for d in range(steps):
        row = jnp.where(lane == WHEN + d, when[d], row)
        row = jnp.where(lane == TAKE + d, take[d], row)
    table[...] = jnp.where(lane == OPERATORS, taken, row)


def place_weights(parts, weight):
    half = weight.shape[-1] // 2
    for n, (real, imag) in enumerate(parts):
        weight[n, :half, :half] = real[...]
        weight[n, :half, half:] = -imag[...]
        weight[n, half:, :half] = imag[...]
        weight[n, half:, half:] = real[...]


def make_blocks(entries, ops_ref, left_ref, right_ref, sum_ref, weight, late_too):
    half = ops_ref.shape[-1]

    def one(at, carry):
        n = at >> 1
        use = jnp.bitwise_and(at, 1)
        packed = entries[0]
        for other, value in enumerate(entries[1:], 1):
            packed = jnp.where(n == other, value, packed)

        @pl.when(use < jnp.bitwise_and(packed, 3))
        def _():
            entry = jnp.bitwise_and(jnp.where(use == 0, packed >> 2, packed >> 10), 255)
            kind = entry >> 6
            p = jnp.bitwise_and(entry >> 3, 7)

            @pl.when(kind != LATE)
            def _():
                op = jnp.bitwise_and(entry, 7)
                stacked = jnp.concatenate([ops_ref[0, op], ops_ref[1, op]], axis=1)
                block = dot(stacked, weight[n], ((1,), (1,))).astype(jnp.bfloat16)

                @pl.when(kind == LEFT)
                def _():
                    left_ref[p] = block

                @pl.when(kind == RIGHT)
                def _():
                    right_ref[p, :half] = block
                    right_ref[p, half:, :half] = -block[:, half:]
                    right_ref[p, half:, half:] = block[:, :half]

            if late_too:

                @pl.when(kind == LATE)
                def _():
                    product = dot(left_ref[p], weight[n], ((1,), (1,)))
                    sum_ref[0] += product[:, :half]
                    sum_ref[1] += product[:, half:]

        return carry

    lax.fori_loop(0, 2 * len(entries), one, 0)


def take_operators(mask, operators, ops_ref, left_ref, weight):
    half = ops_ref.shape[-1]

    def pair(p, carry):
        @pl.when(jnp.bitwise_and(mask >> p, 1) == 1)
        def _():
            op = jnp.bitwise_and(operators >> (3 * p), 7)
            weight[0, :half, :half] = ops_ref[0, op]
            weight[0, :half, half:] = ops_ref[1, op]
            weight[0, half:, :half] = -ops_ref[1, op]
            weight[0, half:, half:] = ops_ref[0, op]
            left_ref[p] = dot(left_ref[p], weight[0], ((1,), (0,))).astype(jnp.bfloat16)

        return carry

    @pl.when(mask > 0)
    def _():
        lax.fori_loop(0, left_ref.shape[0], pair, 0)


def add_pairs(mask, left_ref, right_ref, sum_ref, rows):
    half = sum_ref.shape[-1]

    def pair(p, carry):
        @pl.when(jnp.bitwise_and(mask >> p, 1) == 1)
        def _():
            product = dot(left_ref[p, rows], right_ref[p], ((1,), (0,)))
            sum_ref[0, rows] += product[:, :half]
            sum_ref[1, rows] += product[:, half:]

        return carry

    @pl.when(mask > 0)
    def _():
        lax.fori_loop(0, left_ref.shape[0], pair, 0)


def work(slots, parts, state, ops, step=None, behind=None, final=False, begin=None):
    half = ops.shape[-1]
    smem = pl.BlockSpec(memory_space=pltpu.SMEM)
    vmem = pl.BlockSpec(memory_space=pltpu.VMEM)
    arrays = [array for pair in parts for array in pair if array is not None]
    if begin:
        ids, me, ring = begin
        pairs = ids.shape[0] // 2
        operands, in_specs = [ids, me, ops, *arrays], [smem, smem]
        out_shape = [jax.ShapeDtypeStruct((ROW, LANES), jnp.int32)]
        out_specs, aliases = [vmem, vmem, vmem, vmem], {}
    else:
        pairs = state[1].shape[0]
        operands, in_specs = [state[0], ops, *arrays, *state[1:]], []
        out_shape, out_specs = [], [vmem, vmem, vmem]
        aliases = {2 + len(arrays) + n: n for n in range(3)}
    in_specs += [vmem] * (len(operands) - len(in_specs))
    out_shape += [
        jax.ShapeDtypeStruct((pairs, half, 2 * half), jnp.bfloat16),
        jax.ShapeDtypeStruct((pairs, 2 * half, 2 * half), jnp.bfloat16),
        jax.ShapeDtypeStruct((2, half, half), jnp.float32),
    ]
    scratch = [pltpu.VMEM((len(slots), 2 * half, 2 * half), jnp.bfloat16)]
    chunks = 1
    if begin:
        scratch.append(pltpu.SMEM((SCALARS,), jnp.int32))
    if final:
        out_shape.append(jax.ShapeDtypeStruct((2, half, half), jnp.float32))
        out_specs.append(pl.BlockSpec(memory_space=pl.ANY))
        scratch.append(pltpu.SemaphoreType.DMA((chunks,)))

    def kernel(*refs):
        given = refs[: len(operands)]
        outs = refs[len(operands) : len(operands) + len(out_shape)]
        weight = refs[len(operands) + len(out_shape)]
        if begin:
            ids_ref, me_ref, ops_ref = given[:3]
            at = 3
            table, left_ref, right_ref, sum_ref = outs
            fill_table(table, refs[-1], ids_ref, me_ref[0], ring, ops_ref.shape[1], ids_ref.shape[0])
            sum_ref[...] = jnp.zeros(sum_ref.shape, jnp.float32)
        else:
            ops_ref = given[1]
            at = 2
            table = given[0]
            left_ref, right_ref, sum_ref = outs[:3]
        sources = []
        for pair in parts:
            if pair[1] is None:
                sources.append((given[at].at[0], given[at].at[1]))
                at += 1
            else:
                sources.append((given[at], given[at + 1]))
                at += 2
        row = table[...]
        entries = [row[0, slot] for slot in slots]
        if behind is not None:
            take_operators(row[0, TAKE + behind], row[0, OPERATORS], ops_ref, left_ref, weight)
            add_pairs(row[0, WHEN + behind], left_ref, right_ref, sum_ref, slice(None))
        if step is not None:
            when = row[0, WHEN + step]
            if not final:
                take, operators = row[0, TAKE + step], row[0, OPERATORS]
        place_weights(sources, weight)
        make_blocks(entries, ops_ref, left_ref, right_ref, sum_ref, weight, slots[0] > 1)
        if step is None:
            return
        if not final:
            take_operators(take, operators, ops_ref, left_ref, weight)
            add_pairs(when, left_ref, right_ref, sum_ref, slice(None))
            return
        copies = []
        for n in range(chunks):
            rows = slice(n * half // chunks, (n + 1) * half // chunks)
            add_pairs(when, left_ref, right_ref, sum_ref, rows)
            scale = 1.0 / jnp.sqrt(jnp.float32(2 * half * pairs))
            sum_ref[:, rows] = sum_ref[:, rows] * scale
            copies.append(
                pltpu.make_async_copy(
                    sum_ref.at[:, rows], outs[3].at[:, rows], refs[-1].at[n]
                )
            )
            copies[-1].start()
        for copy in copies:
            copy.wait()

    outs = pl.pallas_call(
        kernel,
        out_shape=tuple(out_shape),
        in_specs=in_specs,
        out_specs=tuple(out_specs),
        scratch_shapes=scratch,
        input_output_aliases=aliases,
        compiler_params=pltpu.CompilerParams(vmem_limit_bytes=LIMIT),
        cost_estimate=pl.CostEstimate(
            flops=len(slots) * 8 * half**3, transcendentals=0, bytes_accessed=len(slots) * 4 * half**2
        ),
        name="work",
    )(*operands)
    if final:
        return outs[3]
    return tuple(outs) if begin else (state[0], *outs)


def placed(perambulator, meson_ops, diagram_lists):
    sa_count = lax.axis_size("sa")
    ring = sa_count // 2
    far = ring // 2

    def hop(value, step):
        return lax.ppermute(value, "sa", [(i, (i + 2 * step) % sa_count) for i in range(sa_count)])

    def swap(value):
        return lax.ppermute(value, "sa", [(i, i ^ 1) for i in range(sa_count)])

    ids = diagram_lists.reshape(-1)
    me = lax.axis_index("sa").astype(jnp.int32).reshape(1)
    ops = meson_ops[:, :, 0]
    owned = lax.all_to_all(perambulator, "ta", split_axis=1, concat_axis=3, tiled=True)[:, 0, 0]
    up = {0: owned}
    down = {0: owned}
    for d in range(1, far):
        up[d] = hop(up[d - 1], 1)
        down[d] = hop(down[d - 1], -1)
    up[far] = hop(up[far - 1][0], 1)
    down[far] = hop(down[far - 1][1], -1)
    state = None
    for d in range(far + 1):
        other_up = swap(up[d])
        other_down = swap(down[d]) if d else None
        if d == far:
            own, other = [(up[d], down[d])], [(other_up, other_down)]
            slots = [2 * d]
        elif d:
            own, other = [(up[d], None), (down[d], None)], [(other_up, None), (other_down, None)]
            slots = [2 * d, 2 * (ring - d)]
        else:
            own, other = [(up[d], None)], [(other_up, None)]
            slots = [0]
        begin = None if d else (ids, me, ring)
        state = work(slots, own, state, ops, behind=d - 1 if d == far else None, begin=begin)
        step = None if d == far - 1 else d
        state = work([s + 1 for s in slots], other, state, ops, step=step, final=d == far)
    return state[:, None, None]


def solution(mesh):
    in_specs = (
        P(None, None, "sa", "ta", None),
        P(None, None, "ta", None, None),
        P("ta", "sa", None),
    )
    out_specs = P(None, "ta", "sa", None, None)
    return jax.shard_map(placed, mesh=mesh, in_specs=in_specs, out_specs=out_specs, check_vma=False)
```
